32 devices in a mesh: row: 4 (over x, core), col: 8 (over z, y).
Axes of the slice: x: 2, y: 2, z: 4, core: 2. Of those that a mesh axis runs over, the one named last changes fastest.
Arguments:
- schur: float32 [4096, 4096], P('row', 'col'), may hold values from -6 to 6
- left_rot: float32 [8, 512, 512], P('row', 'col'), may hold values from -1 to 1, as said below
- right_rot: float32 [8, 512, 512], P('col', 'row'), may hold values from -1 to 1, as said below
- left_off: float32 [8, 512, 512], P('row', 'col'), may hold values from -1 to 1, as said below
- right_off: float32 [8, 512, 512], P('col', 'row'), may hold values from -1 to 1, as said below
Outputs:
- updated: float32 [4096, 4096], P('row', 'col')
The draws below stay inside these ranges and needn't reach their ends.
Inputs may be any that keep to these rules, and one draw needn't show every extreme that they name: `left_rot`: each 512 x 512 block is orthogonal. `right_rot`: each 512 x 512 block is orthogonal. `left_off`: each 512 x 512 block is orthogonal. `right_off`: each 512 x 512 block is orthogonal.
All inputs are finite; a program needn't handle non-finite values.
Results may differ from the reference program's by a relative error of at most 0.00007.
Values sent between devices are 32-bit elements; how exact they have to be, the bound alone decides.
A program may use at most 64 MiB of HBM per device.

```python
import jax
import jax.numpy as jnp
from jax import lax

WIN = 512
NROWS = 4096
NCOLS = 4096
LEFT_WINS = 8
RIGHT_WINS = 8


def orthogonal_blocks(key, number):
    base = jax.random.normal(key, (number, WIN, WIN), jnp.float32)
    factor_q, factor_r = jnp.linalg.qr(base)
    signs = jnp.sign(jnp.diagonal(factor_r, axis1=1, axis2=2)) + 0.0
    signs = jnp.where(signs == 0.0, 1.0, signs)
    return factor_q * signs[:, None, :]


def draw_left_rot(key, part):
    return orthogonal_blocks(jax.random.fold_in(key, 11), LEFT_WINS)


def draw_right_rot(key, part):
    return orthogonal_blocks(jax.random.fold_in(key, 23), RIGHT_WINS)


def draw_left_off(key, part):
    return orthogonal_blocks(jax.random.fold_in(key, 37), LEFT_WINS)


def draw_right_off(key, part):
    return orthogonal_blocks(jax.random.fold_in(key, 41), RIGHT_WINS)


def shard_levels(own_key, extent, cuts, low, top_value):
    level = 1.0
    for axis_at, blocks in cuts:
        draws = jax.random.uniform(jax.random.fold_in(jax.random.fold_in(own_key, 6), axis_at), (blocks,), jnp.float32, low / len(cuts), top_value / len(cuts))
        level = level * jnp.repeat(jnp.exp(draws), extent[axis_at] // blocks).reshape((-1,) + (1,) * (len(extent) - 1 - axis_at))
    return level


def noise(key, shape, deviation, limit, pieces=(), held_as=jnp.bfloat16):
    entries = deviation * jax.random.normal(key, shape, jnp.float32)
    if pieces:
        entries = entries * shard_levels(key, shape, pieces, -0.22, 0.18)
    return jnp.clip(entries, -limit, limit).astype(held_as)


def setup_inputs(seed: int = 0) -> dict:
    key_of = jax.random.split(jax.random.key(seed), 6)
    schur = noise(key_of[0], (NROWS, NCOLS), 1.0, 6.0, ((0, 4), (1, 8)), jnp.float32)
    left_rot = draw_left_rot(jax.random.fold_in(key_of[5], 71), 0)
    right_rot = draw_right_rot(jax.random.fold_in(key_of[5], 71), 0)
    left_off = draw_left_off(jax.random.fold_in(key_of[5], 71), 0)
    right_off = draw_right_off(jax.random.fold_in(key_of[5], 71), 0)
    return {"schur": schur, "left_rot": left_rot, "right_rot": right_rot, "left_off": left_off, "right_off": right_off}


def left_apply(matrix, rotations):
    number = rotations.shape[0]
    window = rotations.shape[1]
    shaped = matrix.reshape(number, window, matrix.shape[1])
    result = jnp.einsum('kab,kac->kbc', rotations, shaped, precision=lax.Precision.HIGHEST)
    return result.reshape(matrix.shape)

def right_apply(matrix, rotations):
    number = rotations.shape[0]
    window = rotations.shape[1]
    shaped = matrix.reshape(matrix.shape[0], number, window)
    result = jnp.einsum('rka,kab->rkb', shaped, rotations, precision=lax.Precision.HIGHEST)
    return result.reshape(matrix.shape)

def reference(schur, left_rot, right_rot, left_off, right_off):
    half_window = WIN // 2
    matrix = left_apply(schur, left_rot)
    matrix = right_apply(matrix, right_rot)
    matrix = jnp.roll(matrix, half_window, axis=0)
    matrix = left_apply(matrix, left_off)
    matrix = jnp.roll(matrix, -half_window, axis=0)
    matrix = jnp.roll(matrix, half_window, axis=1)
    matrix = right_apply(matrix, right_off)
    matrix = jnp.roll(matrix, -half_window, axis=1)
    return matrix
```

```python
import functools

import jax
import jax.numpy as jnp
from jax import lax
from jax.experimental import pallas as pl
from jax.experimental.pallas import tpu as pltpu
from jax.sharding import PartitionSpec as P

MESH = pl.DeviceIdType.MESH
F32 = jnp.float32
BF16 = jnp.bfloat16


def run(pred, fn):
    if pred is None:
        fn()
    else:
        pl.when(pred)(fn)


def both(a, b):
    if a is None:
        return b
    if b is None:
        return a
    return jnp.logical_and(a, b)


def split(v):
    high = v.astype(BF16)
    return high, (v - high.astype(F32)).astype(BF16)


def dot3(a, b, dims):
    def one(p, q):
        return lax.dot_general(p, q, (dims, ((), ())), preferred_element_type=F32)

    return one(a[0], b[0]) + (one(a[0], b[1]) + one(a[1], b[0]))


DETOUR = 0
SHORT = 1
RIGHT = ((1,), (0,))
LEFT = ((0,), (0,))


def kernel(
    R, C, chunk, detour,
    x_in, rr_in, ro_in, lr_in, lo_in, out,
    x, rr, ro, nx, lr, lo, nl, m, m2, m3, hp, hn, hx, ha, hb,
    rr_h, rr_l, ro_h, ro_l, nx_h, nx_l,
    rr_s, rr_r, ro_s, ro_r, nx_s, nx_r, lr_s, lr_r, lo_s, lo_r, nl_s, nl_r,
    hp_s, hp_r, hn_s, hn_r, hx_s, hx_r, hr_s, hr_r, x_s,
):
    r = lax.axis_index("row")
    c = lax.axis_index("col")
    L = C // 2
    line = lax.div(c, 2)
    y = lax.rem(c, 2)
    mate = 2 * line + 1 - y
    c_next, c_prev = lax.rem(c + 1, C), lax.rem(c + C - 1, C)
    r_next, r_prev = lax.rem(r + 1, R), lax.rem(r + R - 1, R)
    can_up, can_down = line < L - 1, line > 0
    in_up, in_down = line < L - 2, line > 1
    at_end = jnp.logical_or(line == 0, line == L - 1)
    c_up, c_down = lax.rem(c + 2, C), lax.rem(c + C - 2, C)
    rows, cols = x.shape
    win = lr_in.shape[2]
    half = win // 2
    nr = rr_in.shape[0]
    nleft = lr_in.shape[0]
    pending = []
    fetch = pltpu.make_async_copy(x_in, x, x_s)
    fetch.start()

    around = functools.reduce(jnp.logical_or, [c == 0, c == 2, c == C - 3, c == C - 1])
    via = jnp.where(c == 0, C - 3, jnp.where(c == 2, 3, jnp.where(c == C - 3, C - 4, 2)))
    low_relay = jnp.logical_or(c == 2, c == 3)
    relays = jnp.logical_or(low_relay, jnp.logical_or(c == C - 4, c == C - 3))
    onward = jnp.where(low_relay, c_down, c_up)

    def put(src, dst, ssem, rsem, dev, pred=None):
        def copy():
            return pltpu.make_async_remote_copy(
                src_ref=src(), dst_ref=dst(), send_sem=ssem(), recv_sem=rsem(),
                device_id=dev, device_id_type=MESH,
            )

        run(pred, lambda: copy().start())
        pending.append((pred, lambda: copy().wait_send()))

    def got(dst, rsem, pred=None):
        def wait():
            pltpu.make_async_remote_copy(
                src_ref=dst(), dst_ref=dst(), send_sem=rsem(), recv_sem=rsem(),
                device_id={"col": c_next}, device_id_type=MESH,
            ).wait_recv()

        run(pred, wait)

    barrier = pltpu.get_barrier_semaphore()

    def greet(dev, pred=None):
        run(pred, lambda: pl.semaphore_signal(barrier, inc=1, device_id=dev, device_id_type=MESH))

    for d in range(1, R):
        greet({"row": lax.rem(r + d, R)})
    greet({"col": c_next})
    greet({"col": c_prev})
    greet({"col": c_up}, can_up)
    greet({"col": c_down}, can_down)
    callers = R + 1 + can_up.astype(jnp.int32) + can_down.astype(jnp.int32)
    if detour:
        for one, other in ((0, C - 3), (C - 1, 2)):
            greet({"col": other}, c == one)
            greet({"col": one}, c == other)
            callers = callers + jnp.logical_or(c == one, c == other).astype(jnp.int32)
    pl.semaphore_wait(barrier, callers)

    peers = [lax.rem(r + 2 * d, R) for d in range(1, R // 2)]
    sib = r + 1 - 2 * lax.rem(r, 2)

    def round_rows(src, buf, ss, rs):
        for d, q in enumerate(peers):
            put(src, lambda: buf.at[r], lambda d=d: ss.at[d], lambda: rs.at[r], {"row": q})
        put(src, lambda: buf.at[r], lambda: ss.at[R // 2 - 1], lambda: rs.at[r], {"row": sib})

    def to_sibling(buf, ss, rs):
        for d, q in enumerate(peers):
            got(lambda: buf.at[q], lambda: rs.at[q])
            put(lambda q=q: buf.at[q], lambda q=q: buf.at[q], lambda d=d: ss.at[R // 2 + d],
                lambda q=q: rs.at[q], {"row": sib})

    def from_sibling(buf, rs):
        for q in [sib] + [lax.rem(sib + 2 * d, R) for d in range(1, R // 2)]:
            got(lambda: buf.at[q], lambda: rs.at[q])

    class Gather:
        def __init__(self, own, buf, ss, rs):
            self.own, self.buf, self.ss, self.rs = own, buf, ss, rs
            self.waited = []

        def send(self, j, w, k, pred, own=False):
            src = (lambda: self.own.at[w]) if own else (lambda: self.buf.at[j, w])
            put(src, lambda: self.buf.at[j, w], lambda: self.ss.at[k, j, w],
                lambda: self.rs.at[j, w], {"col": (c_up, c_down, mate)[k]}, pred)

        def wait(self, j, w, pred=None):
            got(lambda: self.buf.at[j, w], lambda: self.rs.at[j, w], pred)

    lr_g = Gather(lr_in, lr, lr_s, lr_r)
    lo_g = Gather(lo_in, lo, lo_s, lo_r)

    def source(side, d, own):
        plane = line - d if side == 0 else line + d
        has = plane >= 0 if side == 0 else plane <= L - 1
        return lax.rem(2 * plane + (y if own else 1 - y) + 2 * C, C), has

    def onwards(g, side, d, own, w):
        can, inner = ((can_up, in_up), (can_down, in_down))[side]
        j, has = source(side, d, own)
        along = both(has, can if own or g is lr_g else inner)
        across = None
        if own and (g is lo_g or (d == 1 and w < SHORT)):
            across = both(has, at_end)
        return j, has, along, across

    def nl_put(j, pred, own=False):
        src = lo_in.at[0, :, pl.ds(0, half)] if own else None
        put(lambda: src if own else lo.at[j, 0, :, pl.ds(0, half)], lambda: nl.at[j],
            lambda: nl_s.at[j], lambda: nl_r.at[j], {"row": r_prev}, pred)

    def relay(g, d, own, w):
        for side in (0, 1):
            if d == L - 1:
                use = jnp.bool_(False)
            j, has, along, across = onwards(g, side, d, own, w)
            use = along if across is None else jnp.logical_or(along, across)
            if d == L - 1 and across is None:
                continue
            g.wait(j, w, use)
            g.send(j, w, side, along)
            if across is not None:
                g.send(j, w, 2, across)
            if g is lo_g and w == 0:
                nl_put(j, use)

    def settle(g, w):
        for d in range(1, L):
            for own in (True, False):
                for side in (0, 1):
                    j, has, along, across = onwards(g, side, d, own, w)
                    use = along if across is None else jnp.logical_or(along, across)
                    rest = has if d == L - 1 and across is None else both(has, jnp.logical_not(use))
                    g.wait(j, w, rest)
                    if g is lo_g and w == 0:
                        nl_put(j, rest)

    round_rows(lambda: rr_in, rr, rr_s, rr_r)
    for w in range(nleft):
        lr_g.send(c, w, 2, None, True)
        lr_g.send(c, w, 0, can_up, True)
        lr_g.send(c, w, 1, can_down, True)
    put(lambda: ro_in.at[0, :, pl.ds(0, half)], lambda: nx.at[r], lambda: nx_s.at[R - 1],
        lambda: nx_r.at[r], {"col": c_prev})
    round_rows(lambda: ro_in, ro, ro_s, ro_r)
    for w in range(nleft):
        lo_g.send(c, w, 2, None, True)
    nl_put(c, None, True)
    rr[r] = rr_in[...]
    ro[r] = ro_in[...]
    lr[c] = lr_in[...]
    lo[c] = lo_in[...]

    for w in range(nleft):
        lr_g.wait(mate, w)
        lr_g.send(mate, w, 0, in_up if w < SHORT else can_up)
        lr_g.send(mate, w, 1, in_down if w < SHORT else can_down)
        relay(lr_g, 1, True, w)
    to_sibling(rr, rr_s, rr_r)
    from_sibling(rr, rr_r)
    for w in range(nr):
        h, l = split(rr[:, w].reshape(win, win))
        rr_h[w] = h
        rr_l[w] = l
    n_chunks = rows // chunk
    odd = lax.rem(r, 2)

    def turn(i, n):
        return i + odd * (n - 1 - 2 * i)

    def span(i):
        return pl.ds(pl.multiple_of(i * chunk, chunk), chunk)

    def halo(i, forward, n=None):
        cut = pl.ds(cols - half, half) if forward else pl.ds(0, half)
        dst, ss, rs = (hp, hp_s, hp_r) if forward else (hn, hn_s, hn_r)
        if n is None:
            return pltpu.make_async_remote_copy(
                src_ref=m.at[span(i), cut], dst_ref=dst.at[span(i), :],
                send_sem=ss.at[i], recv_sem=rs.at[i],
                device_id={"col": c_next if forward else c_prev}, device_id_type=MESH)
        return pltpu.make_async_remote_copy(
            src_ref=m.at[span(i), cut], dst_ref=hx.at[n],
            send_sem=ss.at[i], recv_sem=hx_r.at[n],
            device_id={"col": via}, device_id_type=MESH)

    def far_start(i, n):
        for forward in (True, False):
            far = y == (1 if forward else 0)
            if n is None:
                run(far, lambda: halo(i, forward).start())
            else:
                run(both(far, around), lambda: halo(i, forward, n).start())
                run(both(far, jnp.logical_not(around)), lambda: halo(i, forward).start())

    def near_start(i):
        for forward in (True, False):
            run(y == (0 if forward else 1), lambda: halo(i, forward).start())

    def right_chunk(i):
        for w in range(nr):
            a = split(x[span(i), pl.ds(w * win, win)])
            m[span(i), pl.ds(w * win, win)] = dot3(a, (rr_h[w], rr_l[w]), RIGHT)

    fetch.wait()
    for n in range(n_chunks):
        i = turn(n, n_chunks)
        right_chunk(i)
        far_start(i, n if n < detour else None)
        if n >= detour:
            near_start(i)
        if n == detour - 1:
            for k in range(detour):
                near_start(turn(k, n_chunks))

    def hx_copy(n):
        i = turn(n, n_chunks)
        even = pltpu.make_async_remote_copy(
            src_ref=hx.at[n], dst_ref=hp.at[span(i), :], send_sem=hx_s.at[n], recv_sem=hp_r.at[i],
            device_id={"col": onward}, device_id_type=MESH)
        uneven = pltpu.make_async_remote_copy(
            src_ref=hx.at[n], dst_ref=hn.at[span(i), :], send_sem=hx_s.at[n], recv_sem=hn_r.at[i],
            device_id={"col": onward}, device_id_type=MESH)
        return even, uneven

    def hx_relay(n):
        got(lambda: hx.at[n], lambda: hx_r.at[n], relays)
        even, uneven = hx_copy(n)
        run(both(relays, y == 0), even.start)
        run(both(relays, y == 1), uneven.start)

    got(lambda: nx.at[r], lambda: nx_r.at[r])
    round_rows(lambda: nx.at[r], nx, nx_s, nx_r)
    for w in range(nleft):
        relay(lr_g, 1, False, w)
    for w in range(nleft):
        lo_g.send(c, w, 0, can_up, True)
        lo_g.send(c, w, 1, can_down, True)
    to_sibling(ro, ro_s, ro_r)
    to_sibling(nx, nx_s, nx_r)
    for n in range(detour):
        hx_relay(n)
    for d in range(2, L):
        for own in (True, False):
            for w in range(nleft):
                relay(lr_g, d, own, w)

    def lo_mate(w):
        lo_g.wait(mate, w)
        lo_g.send(mate, w, 0, in_up)
        lo_g.send(mate, w, 1, in_down)
        if w == 0:
            nl_put(mate, None)

    from_sibling(ro, ro_r)
    from_sibling(nx, nx_r)
    for w in range(nr):
        h, l = split(ro[:, w].reshape(win, win))
        ro_h[w] = h
        ro_l[w] = l
    h, l = split(nx[...].reshape(win, half))
    nx_h[...] = h
    nx_l[...] = l
    for w in range(nleft):
        lo_mate(w)

    def shifted_chunk(i):
        got(lambda: hp.at[span(i), :], lambda: hp_r.at[i])
        first = split(m[span(i), pl.ds(0, half)])
        ahead = split(hp[span(i), :])
        top = (ro_h[0, :half, half:], ro_l[0, :half, half:])
        low = (ro_h[0, half:, half:], ro_l[0, half:, half:])
        m2[span(i), pl.ds(0, half)] = dot3(ahead, top, RIGHT) + dot3(first, low, RIGHT)
        for w in range(1, nr):
            a = split(m[span(i), pl.ds(w * win - half, win)])
            m2[span(i), pl.ds(w * win - half, win)] = dot3(a, (ro_h[w], ro_l[w]), RIGHT)
        got(lambda: hn.at[span(i), :], lambda: hn_r.at[i])
        last = split(m[span(i), pl.ds(cols - half, half)])
        after = split(hn[span(i), :])
        top = (nx_h[:half, :], nx_l[:half, :])
        low = (nx_h[half:, :], nx_l[half:, :])
        m2[span(i), pl.ds(cols - half, half)] = dot3(last, top, RIGHT) + dot3(after, low, RIGHT)

    per = win // chunk

    def left_window(k):
        k = turn(k, nleft)
        at = pl.ds(pl.multiple_of(k * win, win), win)
        q = split(lr[:, k].reshape(win, win))
        for w in range(cols // win):
            across = pl.ds(w * win, win)
            m3[at, across] = dot3(q, split(m2[at, across]), LEFT)

    def rows_up(pred):
        put(lambda: m3.at[pl.ds(rows - half, half), :], lambda: ha, lambda: hr_s.at[0],
            lambda: hr_r.at[0], {"row": r_next}, pred)

    def rows_down(pred):
        put(lambda: m3.at[pl.ds(0, half), :], lambda: hb, lambda: hr_s.at[1],
            lambda: hr_r.at[1], {"row": r_prev}, pred)

    for n in range(per):
        shifted_chunk(turn(n, n_chunks))
    for own in (True, False):
        relay(lo_g, 1, own, 0)
    for w in range(nleft):
        settle(lr_g, w)
    left_window(0)
    rows_down(odd == 0)
    rows_up(odd == 1)
    for w in range(1, nleft):
        for own in (True, False):
            relay(lo_g, 1, own, w)
    for k in range(1, nleft):
        for n in range(k * per, (k + 1) * per):
            shifted_chunk(turn(n, n_chunks))
        left_window(k)
    rows_up(odd == 0)
    rows_down(odd == 1)
    for w in range(nleft):
        for d in range(2, L):
            for own in (True, False):
                relay(lo_g, d, own, w)

    strip = win // C

    def store(q, parts, at, add):
        res = dot3(split(q), split(jnp.concatenate(parts, axis=0)), LEFT)
        out[at, :] = out[at, :] + res if add else res

    settle(lo_g, 0)
    got(lambda: ha, lambda: hr_r.at[0])
    store(lo[:, 0, :, half:].reshape(win, half), [ha[...], m3[pl.ds(0, half), :]],
          pl.ds(0, half), False)
    for j in range(C):
        got(lambda: nl.at[j], lambda: nl_r.at[j])
    got(lambda: hb, lambda: hr_r.at[1])
    store(nl[...].reshape(win, half), [m3[pl.ds(rows - half, half), :], hb[...]],
          pl.ds(rows - half, half), False)
    for w in range(1, nleft):
        settle(lo_g, w)
        base = w * win - half
        store(lo[:, w].reshape(win, win), [m3[pl.ds(base, win), :]], pl.ds(base, win), False)

    for n in range(n_chunks):
        i = turn(n, n_chunks)
        for forward in (True, False):
            halo(i, forward).wait_send()
        if n < detour:
            run(relays, hx_copy(n)[0].wait_send)
    for pred, wait in pending:
        run(pred, wait)


def solution(mesh):
    R, C = mesh.shape["row"], mesh.shape["col"]

    def body(schur, left_rot, right_rot, left_off, right_off):
        rows, cols = schur.shape
        win = left_rot.shape[2]
        half = win // 2
        nr, nleft = right_rot.shape[0], left_rot.shape[0]
        chunk = half
        n_chunks = rows // chunk
        dma = pltpu.SemaphoreType.DMA
        vm = pltpu.VMEM
        right = (R,) + right_rot.shape
        left = (C,) + left_rot.shape
        return pl.pallas_call(
            functools.partial(kernel, R, C, chunk, DETOUR),
            out_shape=jax.ShapeDtypeStruct((rows, cols), F32),
            in_specs=[pl.BlockSpec(memory_space=pl.ANY)] + [pl.BlockSpec(memory_space=vm)] * 4,
            out_specs=pl.BlockSpec(memory_space=vm),
            scratch_shapes=[
                vm((rows, cols), F32), vm(right, F32), vm(right, F32), vm((R, win // R, half), F32),
                vm(left, F32), vm(left, F32), vm((C, win // C, half), F32),
                vm((rows, cols), F32), vm((rows, cols), F32), vm((rows, cols), F32),
                vm((rows, half), F32), vm((rows, half), F32),
                vm((max(DETOUR, 1), chunk, half), F32),
                vm((half, cols), F32), vm((half, cols), F32),
                vm((nr, win, win), BF16), vm((nr, win, win), BF16),
                vm((nr, win, win), BF16), vm((nr, win, win), BF16),
                vm((win, half), BF16), vm((win, half), BF16),
                dma((R,)), dma((R,)), dma((R,)), dma((R,)), dma((R,)), dma((R,)),
                dma((3, C, nleft)), dma((C, nleft)), dma((3, C, nleft)), dma((C, nleft)), dma((C,)), dma((C,)),
                dma((n_chunks,)), dma((n_chunks,)), dma((n_chunks,)), dma((n_chunks,)),
                dma((max(DETOUR, 1),)), dma((max(DETOUR, 1),)),
                dma((2,)), dma((2,)), dma,
            ],
            compiler_params=pltpu.CompilerParams(collective_id=0, has_side_effects=True),
        )(schur, right_rot, right_off, left_rot, left_off)

    return jax.shard_map(
        body,
        mesh=mesh,
        in_specs=(
            P("row", "col"),
            P("row", "col", None),
            P("col", "row", None),
            P("row", "col", None),
            P("col", "row", None),
        ),
        out_specs=P("row", "col"),
        check_vma=False,
    )
```

```python
import functools

import jax
import jax.numpy as jnp
from jax import lax
from jax.experimental import pallas as pl
from jax.experimental.pallas import tpu as pltpu
from jax.sharding import PartitionSpec as P

MESH = pl.DeviceIdType.MESH
F32 = jnp.float32
BF16 = jnp.bfloat16


def run(pred, fn):
    if pred is None:
        fn()
    else:
        pl.when(pred)(fn)


def both(a, b):
    if a is None:
        return b
    if b is None:
        return a
    return jnp.logical_and(a, b)


def split(v):
    high = v.astype(BF16)
    return high, (v - high.astype(F32)).astype(BF16)


def dot3(a, b, dims):
    def one(p, q):
        return lax.dot_general(p, q, (dims, ((), ())), preferred_element_type=F32)

    return one(a[0], b[0]) + (one(a[0], b[1]) + one(a[1], b[0]))


DETOUR = 0
SHORT = 1
RIGHT = ((1,), (0,))
LEFT = ((0,), (0,))


def kernel(
    R, C, chunk, detour,
    x_in, rr_in, ro_in, lr_in, lo_in, out,
    x, rr, ro, nx, lr, lo, nl, m, m2, m3, hp, hn, hx, ha, hb,
    rr_h, rr_l, ro_h, ro_l, nx_h, nx_l,
    rr_s, rr_r, ro_s, ro_r, nx_s, nx_r, lr_s, lr_r, lo_s, lo_r, nl_s, nl_r,
    hp_s, hp_r, hn_s, hn_r, hx_s, hx_r, hr_s, hr_r, x_s, o_s, tok,
):
    r = lax.axis_index("row")
    c = lax.axis_index("col")
    L = C // 2
    line = lax.div(c, 2)
    y = lax.rem(c, 2)
    mate = 2 * line + 1 - y
    c_next, c_prev = lax.rem(c + 1, C), lax.rem(c + C - 1, C)
    r_next, r_prev = lax.rem(r + 1, R), lax.rem(r + R - 1, R)
    can_up, can_down = line < L - 1, line > 0
    in_up, in_down = line < L - 2, line > 1
    at_end = jnp.logical_or(line == 0, line == L - 1)
    c_up, c_down = lax.rem(c + 2, C), lax.rem(c + C - 2, C)
    rows, cols = x.shape
    win = lr_in.shape[2]
    half = win // 2
    nr = rr_in.shape[0]
    nleft = lr_in.shape[0]
    pending = []
    fetch = pltpu.make_async_copy(x_in, x, x_s)
    owns = [pltpu.make_async_copy(a, b, o_s.at[n]) for n, (a, b) in enumerate(
        ((rr_in, rr.at[r]), (ro_in, ro.at[r]), (lr_in, lr.at[c]), (lo_in, lo.at[c])))]
    for copy in [owns[0], fetch] + owns[1:]:
        copy.start()

    around = functools.reduce(jnp.logical_or, [c == 0, c == 2, c == C - 3, c == C - 1])
    via = jnp.where(c == 0, C - 3, jnp.where(c == 2, 3, jnp.where(c == C - 3, C - 4, 2)))
    low_relay = jnp.logical_or(c == 2, c == 3)
    relays = jnp.logical_or(low_relay, jnp.logical_or(c == C - 4, c == C - 3))
    onward = jnp.where(low_relay, c_down, c_up)

    def put(src, dst, ssem, rsem, dev, pred=None):
        def copy():
            return pltpu.make_async_remote_copy(
                src_ref=src(), dst_ref=dst(), send_sem=ssem(), recv_sem=rsem(),
                device_id=dev, device_id_type=MESH,
            )

        run(pred, lambda: copy().start())
        pending.append((pred, lambda: copy().wait_send()))

    def got(dst, rsem, pred=None):
        def wait():
            pltpu.make_async_remote_copy(
                src_ref=dst(), dst_ref=dst(), send_sem=rsem(), recv_sem=rsem(),
                device_id={"col": c_next}, device_id_type=MESH,
            ).wait_recv()

        run(pred, wait)

    barrier = pltpu.get_barrier_semaphore()

    def greet(dev, pred=None):
        run(pred, lambda: pl.semaphore_signal(barrier, inc=1, device_id=dev, device_id_type=MESH))

    first, final = c == 0, c == C - 1
    for d in range(1, R):
        greet({"row": lax.rem(r + d, R)})
    greet({"col": c_next}, jnp.logical_not(final))
    greet({"col": c_prev}, jnp.logical_not(first))
    greet({"col": c_up}, can_up)
    greet({"col": c_down}, can_down)
    callers = R + 1 + jnp.where(can_up, 1, 0) + jnp.where(can_down, 1, 0)
    pl.semaphore_wait(barrier, callers - jnp.where(jnp.logical_or(first, final), 1, 0))

    def word(n, along, heard, c_to):
        run(both(along, heard), lambda: pl.semaphore_wait(tok.at[n], 1))
        run(along, lambda: pl.semaphore_signal(
            tok.at[n], inc=1, device_id={"col": c_to}, device_id_type=MESH))

    def far_ends():
        word(0, both(y == 0, line >= 1), line >= 2, jnp.where(can_up, c_up, mate))
        word(1, both(y == 1, line <= L - 2), line <= L - 3, jnp.where(can_down, c_down, mate))
        run(final, lambda: pl.semaphore_wait(tok.at[0], 1))
        run(first, lambda: pl.semaphore_wait(tok.at[1], 1))

    peers = [lax.rem(r + 2 * d, R) for d in range(1, R // 2)]
    sib = r + 1 - 2 * lax.rem(r, 2)

    def round_rows(src, buf, ss, rs):
        for d, q in enumerate(peers):
            put(src, lambda: buf.at[r], lambda d=d: ss.at[d], lambda: rs.at[r], {"row": q})
        put(src, lambda: buf.at[r], lambda: ss.at[R // 2 - 1], lambda: rs.at[r], {"row": sib})

    def to_sibling(buf, ss, rs):
        for d, q in enumerate(peers):
            got(lambda: buf.at[q], lambda: rs.at[q])
            put(lambda q=q: buf.at[q], lambda q=q: buf.at[q], lambda d=d: ss.at[R // 2 + d],
                lambda q=q: rs.at[q], {"row": sib})

    def from_sibling(buf, rs):
        for q in [sib] + [lax.rem(sib + 2 * d, R) for d in range(1, R // 2)]:
            got(lambda: buf.at[q], lambda: rs.at[q])

    class Gather:
        def __init__(self, own, buf, ss, rs):
            self.own, self.buf, self.ss, self.rs = own, buf, ss, rs
            self.waited = []

        def send(self, j, w, k, pred, own=False):
            src = (lambda: self.own.at[w]) if own else (lambda: self.buf.at[j, w])
            put(src, lambda: self.buf.at[j, w], lambda: self.ss.at[k, j, w],
                lambda: self.rs.at[j, w], {"col": (c_up, c_down, mate)[k]}, pred)

        def wait(self, j, w, pred=None):
            got(lambda: self.buf.at[j, w], lambda: self.rs.at[j, w], pred)

    lr_g = Gather(lr_in, lr, lr_s, lr_r)
    lo_g = Gather(lo_in, lo, lo_s, lo_r)

    def source(side, d, own):
        plane = line - d if side == 0 else line + d
        has = plane >= 0 if side == 0 else plane <= L - 1
        return lax.rem(2 * plane + (y if own else 1 - y) + 2 * C, C), has

    def onwards(g, side, d, own, w):
        can, inner = ((can_up, in_up), (can_down, in_down))[side]
        j, has = source(side, d, own)
        along = both(has, can if own or g is lr_g else inner)
        across = None
        if own and (g is lo_g or (d == 1 and w < SHORT)):
            across = both(has, at_end)
        return j, has, along, across

    def nl_put(j, pred, own=False):
        src = lo_in.at[0, :, pl.ds(0, half)] if own else None
        put(lambda: src if own else lo.at[j, 0, :, pl.ds(0, half)], lambda: nl.at[j],
            lambda: nl_s.at[j], lambda: nl_r.at[j], {"row": r_prev}, pred)

    def relay(g, d, own, w):
        for side in (0, 1):
            if d == L - 1:
                use = jnp.bool_(False)
            j, has, along, across = onwards(g, side, d, own, w)
            use = along if across is None else jnp.logical_or(along, across)
            if d == L - 1 and across is None:
                continue
            g.wait(j, w, use)
            g.send(j, w, side, along)
            if across is not None:
                g.send(j, w, 2, across)
            if g is lo_g and w == 0:
                nl_put(j, use)

    def settle(g, w):
        for d in range(1, L):
            for own in (True, False):
                for side in (0, 1):
                    j, has, along, across = onwards(g, side, d, own, w)
                    use = along if across is None else jnp.logical_or(along, across)
                    rest = has if d == L - 1 and across is None else both(has, jnp.logical_not(use))
                    g.wait(j, w, rest)
                    if g is lo_g and w == 0:
                        nl_put(j, rest)

    round_rows(lambda: rr_in, rr, rr_s, rr_r)
    for w in range(nleft):
        lr_g.send(c, w, 2, None, True)
        lr_g.send(c, w, 0, can_up, True)
        lr_g.send(c, w, 1, can_down, True)
    far_ends()
    put(lambda: ro_in.at[0, :, pl.ds(0, half)], lambda: nx.at[r], lambda: nx_s.at[R - 1],
        lambda: nx_r.at[r], {"col": c_prev})
    round_rows(lambda: ro_in, ro, ro_s, ro_r)
    for w in range(nleft):
        lo_g.send(c, w, 2, None, True)
    nl_put(c, None, True)
    for copy in owns:
        copy.wait()

    for w in range(nleft):
        lr_g.wait(mate, w)
        lr_g.send(mate, w, 0, in_up if w < SHORT else can_up)
        lr_g.send(mate, w, 1, in_down if w < SHORT else can_down)
        relay(lr_g, 1, True, w)
    to_sibling(rr, rr_s, rr_r)
    from_sibling(rr, rr_r)
    for w in range(nr):
        h, l = split(rr[:, w].reshape(win, win))
        rr_h[w] = h
        rr_l[w] = l
    n_chunks = rows // chunk
    odd = lax.rem(r, 2)

    def turn(i, n):
        return i + odd * (n - 1 - 2 * i)

    def span(i):
        return pl.ds(pl.multiple_of(i * chunk, chunk), chunk)

    def halo(i, forward, n=None):
        cut = pl.ds(cols - half, half) if forward else pl.ds(0, half)
        dst, ss, rs = (hp, hp_s, hp_r) if forward else (hn, hn_s, hn_r)
        if n is None:
            return pltpu.make_async_remote_copy(
                src_ref=m.at[span(i), cut], dst_ref=dst.at[span(i), :],
                send_sem=ss.at[i], recv_sem=rs.at[i],
                device_id={"col": c_next if forward else c_prev}, device_id_type=MESH)
        return pltpu.make_async_remote_copy(
            src_ref=m.at[span(i), cut], dst_ref=hx.at[n],
            send_sem=ss.at[i], recv_sem=hx_r.at[n],
            device_id={"col": via}, device_id_type=MESH)

    def far_start(i, n):
        for forward in (True, False):
            far = y == (1 if forward else 0)
            if n is None:
                run(far, lambda: halo(i, forward).start())
            else:
                run(both(far, around), lambda: halo(i, forward, n).start())
                run(both(far, jnp.logical_not(around)), lambda: halo(i, forward).start())

    def near_start(i):
        for forward in (True, False):
            run(y == (0 if forward else 1), lambda: halo(i, forward).start())

    def right_chunk(i):
        for w in range(nr):
            a = split(x[span(i), pl.ds(w * win, win)])
            m[span(i), pl.ds(w * win, win)] = dot3(a, (rr_h[w], rr_l[w]), RIGHT)

    fetch.wait()
    for n in range(n_chunks):
        i = turn(n, n_chunks)
        right_chunk(i)
        far_start(i, n if n < detour else None)
        if n >= detour:
            near_start(i)
        if n == detour - 1:
            for k in range(detour):
                near_start(turn(k, n_chunks))

    def hx_copy(n):
        i = turn(n, n_chunks)
        even = pltpu.make_async_remote_copy(
            src_ref=hx.at[n], dst_ref=hp.at[span(i), :], send_sem=hx_s.at[n], recv_sem=hp_r.at[i],
            device_id={"col": onward}, device_id_type=MESH)
        uneven = pltpu.make_async_remote_copy(
            src_ref=hx.at[n], dst_ref=hn.at[span(i), :], send_sem=hx_s.at[n], recv_sem=hn_r.at[i],
            device_id={"col": onward}, device_id_type=MESH)
        return even, uneven

    def hx_relay(n):
        got(lambda: hx.at[n], lambda: hx_r.at[n], relays)
        even, uneven = hx_copy(n)
        run(both(relays, y == 0), even.start)
        run(both(relays, y == 1), uneven.start)

    got(lambda: nx.at[r], lambda: nx_r.at[r])
    round_rows(lambda: nx.at[r], nx, nx_s, nx_r)
    for w in range(nleft):
        relay(lr_g, 1, False, w)
    for w in range(nleft):
        lo_g.send(c, w, 0, can_up, True)
        lo_g.send(c, w, 1, can_down, True)
    to_sibling(ro, ro_s, ro_r)
    to_sibling(nx, nx_s, nx_r)
    for n in range(detour):
        hx_relay(n)
    for d in range(2, L):
        for own in (True, False):
            for w in range(nleft):
                relay(lr_g, d, own, w)

    def lo_mate(w):
        lo_g.wait(mate, w)
        lo_g.send(mate, w, 0, in_up)
        lo_g.send(mate, w, 1, in_down)
        if w == 0:
            nl_put(mate, None)

    from_sibling(ro, ro_r)
    from_sibling(nx, nx_r)
    for w in range(nr):
        h, l = split(ro[:, w].reshape(win, win))
        ro_h[w] = h
        ro_l[w] = l
    h, l = split(nx[...].reshape(win, half))
    nx_h[...] = h
    nx_l[...] = l
    for w in range(nleft):
        lo_mate(w)

    def shifted_chunk(i):
        got(lambda: hp.at[span(i), :], lambda: hp_r.at[i])
        first = split(m[span(i), pl.ds(0, half)])
        ahead = split(hp[span(i), :])
        top = (ro_h[0, :half, half:], ro_l[0, :half, half:])
        low = (ro_h[0, half:, half:], ro_l[0, half:, half:])
        m2[span(i), pl.ds(0, half)] = dot3(ahead, top, RIGHT) + dot3(first, low, RIGHT)
        for w in range(1, nr):
            a = split(m[span(i), pl.ds(w * win - half, win)])
            m2[span(i), pl.ds(w * win - half, win)] = dot3(a, (ro_h[w], ro_l[w]), RIGHT)
        got(lambda: hn.at[span(i), :], lambda: hn_r.at[i])
        last = split(m[span(i), pl.ds(cols - half, half)])
        after = split(hn[span(i), :])
        top = (nx_h[:half, :], nx_l[:half, :])
        low = (nx_h[half:, :], nx_l[half:, :])
        m2[span(i), pl.ds(cols - half, half)] = dot3(last, top, RIGHT) + dot3(after, low, RIGHT)

    per = win // chunk

    def left_window(k):
        k = turn(k, nleft)
        at = pl.ds(pl.multiple_of(k * win, win), win)
        q = split(lr[:, k].reshape(win, win))
        for w in range(cols // win):
            across = pl.ds(w * win, win)
            m3[at, across] = dot3(q, split(m2[at, across]), LEFT)

    def rows_up(pred):
        put(lambda: m3.at[pl.ds(rows - half, half), :], lambda: ha, lambda: hr_s.at[0],
            lambda: hr_r.at[0], {"row": r_next}, pred)

    def rows_down(pred):
        put(lambda: m3.at[pl.ds(0, half), :], lambda: hb, lambda: hr_s.at[1],
            lambda: hr_r.at[1], {"row": r_prev}, pred)

    for n in range(per):
        shifted_chunk(turn(n, n_chunks))
    for own in (True, False):
        relay(lo_g, 1, own, 0)
    for w in range(nleft):
        settle(lr_g, w)
    left_window(0)
    rows_down(odd == 0)
    rows_up(odd == 1)
    for w in range(1, nleft):
        for own in (True, False):
            relay(lo_g, 1, own, w)
    for k in range(1, nleft):
        for n in range(k * per, (k + 1) * per):
            shifted_chunk(turn(n, n_chunks))
        left_window(k)
    rows_up(odd == 0)
    rows_down(odd == 1)
    for w in range(nleft):
        for d in range(2, L):
            for own in (True, False):
                relay(lo_g, d, own, w)

    strip = win // C

    def store(q, parts, at, add):
        res = dot3(split(q), split(jnp.concatenate(parts, axis=0)), LEFT)
        out[at, :] = out[at, :] + res if add else res

    settle(lo_g, 0)
    got(lambda: ha, lambda: hr_r.at[0])
    store(lo[:, 0, :, half:].reshape(win, half), [ha[...], m3[pl.ds(0, half), :]],
          pl.ds(0, half), False)
    for j in range(C):
        got(lambda: nl.at[j], lambda: nl_r.at[j])
    got(lambda: hb, lambda: hr_r.at[1])
    store(nl[...].reshape(win, half), [m3[pl.ds(rows - half, half), :], hb[...]],
          pl.ds(rows - half, half), False)
    for w in range(1, nleft):
        settle(lo_g, w)
        base = w * win - half
        store(lo[:, w].reshape(win, win), [m3[pl.ds(base, win), :]], pl.ds(base, win), False)

    for n in range(n_chunks):
        i = turn(n, n_chunks)
        for forward in (True, False):
            halo(i, forward).wait_send()
        if n < detour:
            run(relays, hx_copy(n)[0].wait_send)
    for pred, wait in pending:
        run(pred, wait)


def solution(mesh):
    R, C = mesh.shape["row"], mesh.shape["col"]

    def body(schur, left_rot, right_rot, left_off, right_off):
        rows, cols = schur.shape
        win = left_rot.shape[2]
        half = win // 2
        nr, nleft = right_rot.shape[0], left_rot.shape[0]
        chunk = half
        n_chunks = rows // chunk
        dma = pltpu.SemaphoreType.DMA
        vm = pltpu.VMEM
        right = (R,) + right_rot.shape
        left = (C,) + left_rot.shape
        return pl.pallas_call(
            functools.partial(kernel, R, C, chunk, DETOUR),
            out_shape=jax.ShapeDtypeStruct((rows, cols), F32),
            in_specs=[pl.BlockSpec(memory_space=pltpu.HBM)] * 5,
            out_specs=pl.BlockSpec(memory_space=vm),
            scratch_shapes=[
                vm((rows, cols), F32), vm(right, F32), vm(right, F32), vm((R, win // R, half), F32),
                vm(left, F32), vm(left, F32), vm((C, win // C, half), F32),
                vm((rows, cols), F32), vm((rows, cols), F32), vm((rows, cols), F32),
                vm((rows, half), F32), vm((rows, half), F32),
                vm((max(DETOUR, 1), chunk, half), F32),
                vm((half, cols), F32), vm((half, cols), F32),
                vm((nr, win, win), BF16), vm((nr, win, win), BF16),
                vm((nr, win, win), BF16), vm((nr, win, win), BF16),
                vm((win, half), BF16), vm((win, half), BF16),
                dma((R,)), dma((R,)), dma((R,)), dma((R,)), dma((R,)), dma((R,)),
                dma((3, C, nleft)), dma((C, nleft)), dma((3, C, nleft)), dma((C, nleft)), dma((C,)), dma((C,)),
                dma((n_chunks,)), dma((n_chunks,)), dma((n_chunks,)), dma((n_chunks,)),
                dma((max(DETOUR, 1),)), dma((max(DETOUR, 1),)),
                dma((2,)), dma((2,)), dma, dma((4,)), pltpu.SemaphoreType.REGULAR((2,)),
            ],
            compiler_params=pltpu.CompilerParams(collective_id=0, has_side_effects=True),
        )(schur, right_rot, right_off, left_rot, left_off)

    return jax.shard_map(
        body,
        mesh=mesh,
        in_specs=(
            P("row", "col"),
            P("row", "col", None),
            P("col", "row", None),
            P("row", "col", None),
            P("col", "row", None),
        ),
        out_specs=P("row", "col"),
        check_vma=False,
    )
```

```python
import functools

import jax
import jax.numpy as jnp
from jax import lax
from jax.experimental import pallas as pl
from jax.experimental.pallas import tpu as pltpu
from jax.sharding import PartitionSpec as P

MESH = pl.DeviceIdType.MESH
F32 = jnp.float32
BF16 = jnp.bfloat16


def run(pred, fn):
    if pred is None:
        fn()
    else:
        pl.when(pred)(fn)


def both(a, b):
    if a is None:
        return b
    if b is None:
        return a
    return jnp.logical_and(a, b)


def split(v):
    high = v.astype(BF16)
    return high, (v - high.astype(F32)).astype(BF16)


def dot3(a, b, dims):
    def one(p, q):
        return lax.dot_general(p, q, (dims, ((), ())), preferred_element_type=F32)

    return one(a[0], b[0]) + (one(a[0], b[1]) + one(a[1], b[0]))


DETOUR = 0
SHORT = 1
RIGHT = ((1,), (0,))
LEFT = ((0,), (0,))


def kernel(
    R, C, chunk, detour,
    x_in, rr_in, ro_in, lr_in, lo_in, out,
    x, rr, ro, nx, lr, lo, nl, m, m2, m3, hp, hn, hx, ha, hb,
    rr_h, rr_l, ro_h, ro_l, nx_h, nx_l,
    rr_s, rr_r, ro_s, ro_r, nx_s, nx_r, lr_s, lr_r, lo_s, lo_r, nl_s, nl_r,
    hp_s, hp_r, hn_s, hn_r, hx_s, hx_r, hr_s, hr_r, x_s, o_s, tok,
):
    r = lax.axis_index("row")
    c = lax.axis_index("col")
    L = C // 2
    line = lax.div(c, 2)
    y = lax.rem(c, 2)
    mate = 2 * line + 1 - y
    c_next, c_prev = lax.rem(c + 1, C), lax.rem(c + C - 1, C)
    r_next, r_prev = lax.rem(r + 1, R), lax.rem(r + R - 1, R)
    can_up, can_down = line < L - 1, line > 0
    in_up, in_down = line < L - 2, line > 1
    at_end = jnp.logical_or(line == 0, line == L - 1)
    c_up, c_down = lax.rem(c + 2, C), lax.rem(c + C - 2, C)
    rows, cols = x.shape
    win = lr_in.shape[2]
    half = win // 2
    nr = rr_in.shape[0]
    nleft = lr_in.shape[0]
    pending = []
    fetch = pltpu.make_async_copy(x_in, x, x_s)
    owns = [pltpu.make_async_copy(a, b, o_s.at[n]) for n, (a, b) in enumerate(
        ((rr_in, rr.at[r]), (ro_in, ro.at[r]), (lr_in, lr.at[c]), (lo_in, lo.at[c])))]
    for copy in [owns[0], fetch] + owns[1:]:
        copy.start()

    around = functools.reduce(jnp.logical_or, [c == 0, c == 2, c == C - 3, c == C - 1])
    via = jnp.where(c == 0, C - 3, jnp.where(c == 2, 3, jnp.where(c == C - 3, C - 4, 2)))
    low_relay = jnp.logical_or(c == 2, c == 3)
    relays = jnp.logical_or(low_relay, jnp.logical_or(c == C - 4, c == C - 3))
    onward = jnp.where(low_relay, c_down, c_up)

    def put(src, dst, ssem, rsem, dev, pred=None):
        def copy():
            return pltpu.make_async_remote_copy(
                src_ref=src(), dst_ref=dst(), send_sem=ssem(), recv_sem=rsem(),
                device_id=dev, device_id_type=MESH,
            )

        run(pred, lambda: copy().start())
        pending.append((pred, lambda: copy().wait_send()))

    def got(dst, rsem, pred=None):
        def wait():
            pltpu.make_async_remote_copy(
                src_ref=dst(), dst_ref=dst(), send_sem=rsem(), recv_sem=rsem(),
                device_id={"col": c_next}, device_id_type=MESH,
            ).wait_recv()

        run(pred, wait)

    barrier = pltpu.get_barrier_semaphore()

    def greet(dev, pred=None):
        run(pred, lambda: pl.semaphore_signal(barrier, inc=1, device_id=dev, device_id_type=MESH))

    first, final = c == 0, c == C - 1
    for d in range(1, R):
        greet({"row": lax.rem(r + d, R)})
    greet({"col": c_next}, jnp.logical_not(final))
    greet({"col": c_prev}, jnp.logical_not(first))
    greet({"col": c_up}, can_up)
    greet({"col": c_down}, can_down)
    callers = R + 1 + jnp.where(can_up, 1, 0) + jnp.where(can_down, 1, 0)
    pl.semaphore_wait(barrier, callers - jnp.where(jnp.logical_or(first, final), 1, 0))

    def word(n, along, heard, c_to):
        run(both(along, heard), lambda: pl.semaphore_wait(tok.at[n], 1))
        run(along, lambda: pl.semaphore_signal(
            tok.at[n], inc=1, device_id={"col": c_to}, device_id_type=MESH))

    def far_ends():
        word(0, both(y == 0, line >= 1), line >= 2, jnp.where(can_up, c_up, mate))
        word(1, both(y == 1, line <= L - 2), line <= L - 3, jnp.where(can_down, c_down, mate))
        run(final, lambda: pl.semaphore_wait(tok.at[0], 1))
        run(first, lambda: pl.semaphore_wait(tok.at[1], 1))

    peers = [lax.rem(r + 2 * d, R) for d in range(1, R // 2)]
    sib = r + 1 - 2 * lax.rem(r, 2)

    def round_rows(src, buf, ss, rs):
        for d, q in enumerate(peers):
            put(src, lambda: buf.at[r], lambda d=d: ss.at[d], lambda: rs.at[r], {"row": q})
        put(src, lambda: buf.at[r], lambda: ss.at[R // 2 - 1], lambda: rs.at[r], {"row": sib})

    def to_sibling(buf, ss, rs):
        for d, q in enumerate(peers):
            got(lambda: buf.at[q], lambda: rs.at[q])
            put(lambda q=q: buf.at[q], lambda q=q: buf.at[q], lambda d=d: ss.at[R // 2 + d],
                lambda q=q: rs.at[q], {"row": sib})

    def from_sibling(buf, rs):
        for q in [sib] + [lax.rem(sib + 2 * d, R) for d in range(1, R // 2)]:
            got(lambda: buf.at[q], lambda: rs.at[q])

    class Gather:
        def __init__(self, own, buf, ss, rs):
            self.own, self.buf, self.ss, self.rs = own, buf, ss, rs
            self.waited = []

        def send(self, j, w, k, pred, own=False):
            src = (lambda: self.own.at[w]) if own else (lambda: self.buf.at[j, w])
            put(src, lambda: self.buf.at[j, w], lambda: self.ss.at[k, j, w],
                lambda: self.rs.at[j, w], {"col": (c_up, c_down, mate)[k]}, pred)

        def wait(self, j, w, pred=None):
            got(lambda: self.buf.at[j, w], lambda: self.rs.at[j, w], pred)

    lr_g = Gather(lr_in, lr, lr_s, lr_r)
    lo_g = Gather(lo_in, lo, lo_s, lo_r)

    def source(side, d, own):
        plane = line - d if side == 0 else line + d
        has = plane >= 0 if side == 0 else plane <= L - 1
        return lax.rem(2 * plane + (y if own else 1 - y) + 2 * C, C), has

    def onwards(g, side, d, own, w):
        can, inner = ((can_up, in_up), (can_down, in_down))[side]
        j, has = source(side, d, own)
        along = both(has, can if own or g is lr_g else inner)
        across = None
        if own and (g is lo_g or (d == 1 and w < SHORT)):
            across = both(has, at_end)
        return j, has, along, across

    def nl_put(j, pred, own=False):
        src = lo_in.at[0, :, pl.ds(0, half)] if own else None
        put(lambda: src if own else lo.at[j, 0, :, pl.ds(0, half)], lambda: nl.at[j],
            lambda: nl_s.at[j], lambda: nl_r.at[j], {"row": r_prev}, pred)

    def relay(g, d, own, w):
        for side in (0, 1):
            if d == L - 1:
                use = jnp.bool_(False)
            j, has, along, across = onwards(g, side, d, own, w)
            use = along if across is None else jnp.logical_or(along, across)
            if d == L - 1 and across is None:
                continue
            g.wait(j, w, use)
            g.send(j, w, side, along)
            if across is not None:
                g.send(j, w, 2, across)
            if g is lo_g and w == 0:
                nl_put(j, use)

    def settle(g, w):
        for d in range(1, L):
            for own in (True, False):
                for side in (0, 1):
                    j, has, along, across = onwards(g, side, d, own, w)
                    use = along if across is None else jnp.logical_or(along, across)
                    rest = has if d == L - 1 and across is None else both(has, jnp.logical_not(use))
                    g.wait(j, w, rest)
                    if g is lo_g and w == 0:
                        nl_put(j, rest)

    round_rows(lambda: rr_in, rr, rr_s, rr_r)
    for w in range(nleft):
        lr_g.send(c, w, 2, None, True)
        lr_g.send(c, w, 0, can_up, True)
        lr_g.send(c, w, 1, can_down, True)
    far_ends()
    put(lambda: ro_in.at[0, :, pl.ds(0, half)], lambda: nx.at[r], lambda: nx_s.at[R - 1],
        lambda: nx_r.at[r], {"col": c_prev})
    round_rows(lambda: ro_in, ro, ro_s, ro_r)
    for w in range(nleft):
        lo_g.send(c, w, 2, None, True)
    nl_put(c, None, True)
    for copy in owns:
        copy.wait()

    for w in range(nleft):
        lr_g.wait(mate, w)
        lr_g.send(mate, w, 0, in_up if w < SHORT else can_up)
        lr_g.send(mate, w, 1, in_down if w < SHORT else can_down)
        relay(lr_g, 1, True, w)
    to_sibling(rr, rr_s, rr_r)
    from_sibling(rr, rr_r)
    for w in range(nr):
        h, l = split(rr[:, w].reshape(win, win))
        rr_h[w] = h
        rr_l[w] = l
    n_chunks = rows // chunk
    odd = lax.rem(r, 2)

    def turn(i, n):
        return i + odd * (n - 1 - 2 * i)

    def span(i):
        return pl.ds(pl.multiple_of(i * chunk, chunk), chunk)

    def halo(i, forward, n=None):
        cut = pl.ds(cols - half, half) if forward else pl.ds(0, half)
        dst, ss, rs = (hp, hp_s, hp_r) if forward else (hn, hn_s, hn_r)
        if n is None:
            return pltpu.make_async_remote_copy(
                src_ref=m.at[span(i), cut], dst_ref=dst.at[span(i), :],
                send_sem=ss.at[i], recv_sem=rs.at[i],
                device_id={"col": c_next if forward else c_prev}, device_id_type=MESH)
        return pltpu.make_async_remote_copy(
            src_ref=m.at[span(i), cut], dst_ref=hx.at[n],
            send_sem=ss.at[i], recv_sem=hx_r.at[n],
            device_id={"col": via}, device_id_type=MESH)

    def far_start(i, n):
        for forward in (True, False):
            far = y == (1 if forward else 0)
            if n is None:
                run(far, lambda: halo(i, forward).start())
            else:
                run(both(far, around), lambda: halo(i, forward, n).start())
                run(both(far, jnp.logical_not(around)), lambda: halo(i, forward).start())

    def near_start(i):
        for forward in (True, False):
            run(y == (0 if forward else 1), lambda: halo(i, forward).start())

    def right_chunk(i):
        for w in range(nr):
            a = split(x[span(i), pl.ds(w * win, win)])
            m[span(i), pl.ds(w * win, win)] = dot3(a, (rr_h[w], rr_l[w]), RIGHT)

    fetch.wait()
    for n in range(n_chunks):
        i = turn(n, n_chunks)
        right_chunk(i)
        far_start(i, n if n < detour else None)
        if n >= detour:
            near_start(i)
        if n == detour - 1:
            for k in range(detour):
                near_start(turn(k, n_chunks))

    def hx_copy(n):
        i = turn(n, n_chunks)
        even = pltpu.make_async_remote_copy(
            src_ref=hx.at[n], dst_ref=hp.at[span(i), :], send_sem=hx_s.at[n], recv_sem=hp_r.at[i],
            device_id={"col": onward}, device_id_type=MESH)
        uneven = pltpu.make_async_remote_copy(
            src_ref=hx.at[n], dst_ref=hn.at[span(i), :], send_sem=hx_s.at[n], recv_sem=hn_r.at[i],
            device_id={"col": onward}, device_id_type=MESH)
        return even, uneven

    def hx_relay(n):
        got(lambda: hx.at[n], lambda: hx_r.at[n], relays)
        even, uneven = hx_copy(n)
        run(both(relays, y == 0), even.start)
        run(both(relays, y == 1), uneven.start)

    got(lambda: nx.at[r], lambda: nx_r.at[r])
    round_rows(lambda: nx.at[r], nx, nx_s, nx_r)
    for w in range(nleft):
        relay(lr_g, 1, False, w)
    for w in range(nleft):
        lo_g.send(c, w, 0, can_up, True)
        lo_g.send(c, w, 1, can_down, True)
    to_sibling(ro, ro_s, ro_r)
    to_sibling(nx, nx_s, nx_r)
    for n in range(detour):
        hx_relay(n)
    for d in range(2, L):
        for own in (True, False):
            for w in range(nleft):
                relay(lr_g, d, own, w)

    def lo_mate(w):
        lo_g.wait(mate, w)
        lo_g.send(mate, w, 0, in_up)
        lo_g.send(mate, w, 1, in_down)
        if w == 0:
            nl_put(mate, None)

    from_sibling(ro, ro_r)
    from_sibling(nx, nx_r)
    for w in range(nr):
        h, l = split(ro[:, w].reshape(win, win))
        ro_h[w] = h
        ro_l[w] = l
    h, l = split(nx[...].reshape(win, half))
    nx_h[...] = h
    nx_l[...] = l
    for w in range(nleft):
        lo_mate(w)

    def shifted_chunk(i):
        got(lambda: hp.at[span(i), :], lambda: hp_r.at[i])
        first = split(m[span(i), pl.ds(0, half)])
        ahead = split(hp[span(i), :])
        top = (ro_h[0, :half, half:], ro_l[0, :half, half:])
        low = (ro_h[0, half:, half:], ro_l[0, half:, half:])
        m2[span(i), pl.ds(0, half)] = dot3(ahead, top, RIGHT) + dot3(first, low, RIGHT)
        for w in range(1, nr):
            a = split(m[span(i), pl.ds(w * win - half, win)])
            m2[span(i), pl.ds(w * win - half, win)] = dot3(a, (ro_h[w], ro_l[w]), RIGHT)
        got(lambda: hn.at[span(i), :], lambda: hn_r.at[i])
        last = split(m[span(i), pl.ds(cols - half, half)])
        after = split(hn[span(i), :])
        top = (nx_h[:half, :], nx_l[:half, :])
        low = (nx_h[half:, :], nx_l[half:, :])
        m2[span(i), pl.ds(cols - half, half)] = dot3(last, top, RIGHT) + dot3(after, low, RIGHT)

    per = win // chunk

    def left_window(k):
        k = turn(k, nleft)
        at = pl.ds(pl.multiple_of(k * win, win), win)
        q = split(lr[:, k].reshape(win, win))
        for w in range(cols // win):
            across = pl.ds(w * win, win)
            m3[at, across] = dot3(q, split(m2[at, across]), LEFT)

    def rows_up(pred):
        put(lambda: m3.at[pl.ds(rows - half, half), :], lambda: ha, lambda: hr_s.at[0],
            lambda: hr_r.at[0], {"row": r_next}, pred)

    def rows_down(pred):
        put(lambda: m3.at[pl.ds(0, half), :], lambda: hb, lambda: hr_s.at[1],
            lambda: hr_r.at[1], {"row": r_prev}, pred)

    for n in range(per):
        shifted_chunk(turn(n, n_chunks))
    for own in (True, False):
        relay(lo_g, 1, own, 0)
    for w in range(nleft):
        settle(lr_g, w)
    left_window(0)
    rows_down(odd == 0)
    rows_up(odd == 1)
    for w in range(1, nleft):
        for own in (True, False):
            relay(lo_g, 1, own, w)
    for k in range(1, nleft):
        for n in range(k * per, (k + 1) * per):
            shifted_chunk(turn(n, n_chunks))
        left_window(k)
    rows_up(odd == 0)
    rows_down(odd == 1)
    for w in range(nleft):
        for d in range(2, L):
            for own in (True, False):
                relay(lo_g, d, own, w)

    strip = win // C

    def store(q, parts, at, add):
        res = dot3(split(q), split(jnp.concatenate(parts, axis=0)), LEFT)
        out[at, :] = out[at, :] + res if add else res

    settle(lo_g, 0)
    got(lambda: ha, lambda: hr_r.at[0])
    store(lo[:, 0, :, half:].reshape(win, half), [ha[...], m3[pl.ds(0, half), :]],
          pl.ds(0, half), False)
    for j in range(C):
        got(lambda: nl.at[j], lambda: nl_r.at[j])
    got(lambda: hb, lambda: hr_r.at[1])
    store(nl[...].reshape(win, half), [m3[pl.ds(rows - half, half), :], hb[...]],
          pl.ds(rows - half, half), False)
    for w in range(1, nleft):
        settle(lo_g, w)
        base = w * win - half
        store(lo[:, w].reshape(win, win), [m3[pl.ds(base, win), :]], pl.ds(base, win), False)

    for n in range(n_chunks):
        i = turn(n, n_chunks)
        for forward in (True, False):
            halo(i, forward).wait_send()
        if n < detour:
            run(relays, hx_copy(n)[0].wait_send)
    for pred, wait in pending:
        run(pred, wait)


def solution(mesh):
    R, C = mesh.shape["row"], mesh.shape["col"]

    def body(schur, left_rot, right_rot, left_off, right_off):
        rows, cols = schur.shape
        win = left_rot.shape[2]
        half = win // 2
        nr, nleft = right_rot.shape[0], left_rot.shape[0]
        chunk = half
        n_chunks = rows // chunk
        dma = pltpu.SemaphoreType.DMA
        vm = pltpu.VMEM
        right = (R,) + right_rot.shape
        left = (C,) + left_rot.shape
        return pl.pallas_call(
            functools.partial(kernel, R, C, chunk, DETOUR),
            out_shape=jax.ShapeDtypeStruct((rows, cols), F32),
            in_specs=[pl.BlockSpec(memory_space=pltpu.HBM)] * 5,
            out_specs=pl.BlockSpec(memory_space=vm),
            scratch_shapes=[
                vm((rows, cols), F32), vm(right, F32), vm(right, F32), vm((R, win // R, half), F32),
                vm(left, F32), vm(left, F32), vm((C, win // C, half), F32),
                vm((rows, cols), F32), vm((rows, cols), F32), vm((rows, cols), F32),
                vm((rows, half), F32), vm((rows, half), F32),
                vm((max(DETOUR, 1), chunk, half), F32),
                vm((half, cols), F32), vm((half, cols), F32),
                vm((nr, win, win), BF16), vm((nr, win, win), BF16),
                vm((nr, win, win), BF16), vm((nr, win, win), BF16),
                vm((win, half), BF16), vm((win, half), BF16),
                dma((R,)), dma((R,)), dma((R,)), dma((R,)), dma((R,)), dma((R,)),
                dma((3, C, nleft)), dma((C, nleft)), dma((3, C, nleft)), dma((C, nleft)), dma((C,)), dma((C,)),
                dma((n_chunks,)), dma((n_chunks,)), dma((n_chunks,)), dma((n_chunks,)),
                dma((max(DETOUR, 1),)), dma((max(DETOUR, 1),)),
                dma((2,)), dma((2,)), dma, dma((4,)), pltpu.SemaphoreType.REGULAR((2,)),
            ],
            compiler_params=pltpu.CompilerParams(collective_id=0, has_side_effects=True, vmem_limit_bytes=44 * 2**20),
        )(*(pltpu.with_memory_space_constraint(a, pltpu.HBM) for a in (schur, right_rot, right_off, left_rot, left_off)))

    return jax.shard_map(
        body,
        mesh=mesh,
        in_specs=(
            P("row", "col"),
            P("row", "col", None),
            P("col", "row", None),
            P("row", "col", None),
            P("col", "row", None),
        ),
        out_specs=P("row", "col"),
        check_vma=False,
    )
```

```python
import functools

import jax
import jax.numpy as jnp
from jax import lax
from jax.experimental import pallas as pl
from jax.experimental.pallas import tpu as pltpu
from jax.sharding import PartitionSpec as P

MESH = pl.DeviceIdType.MESH
F32 = jnp.float32
BF16 = jnp.bfloat16


def run(pred, fn):
    if pred is None:
        fn()
    else:
        pl.when(pred)(fn)


def both(a, b):
    if a is None:
        return b
    if b is None:
        return a
    return jnp.logical_and(a, b)


def split(v):
    high = v.astype(BF16)
    return high, (v - high.astype(F32)).astype(BF16)


def dot3(a, b, dims):
    def one(p, q):
        return lax.dot_general(p, q, (dims, ((), ())), preferred_element_type=F32)

    return one(a[0], b[0]) + (one(a[0], b[1]) + one(a[1], b[0]))


DETOUR = 0
SHORT = 1
DIRECT = 1
RIGHT = ((1,), (0,))
LEFT = ((0,), (0,))


def kernel(
    R, C, chunk, detour,
    x_in, rr_in, ro_in, lr_in, lo_in, out,
    x, rr, ro, nx, lr, lo, nl, m, m2, m3, hp, hn, hx, ha, hb,
    rr_h, rr_l, ro_h, ro_l, nx_h, nx_l,
    rr_s, rr_r, ro_s, ro_r, nx_s, nx_r, lr_s, lr_r, lo_s, lo_r, nl_s, nl_r,
    hp_s, hp_r, hn_s, hn_r, hx_s, hx_r, hr_s, hr_r, x_s, o_s, tok,
):
    r = lax.axis_index("row")
    c = lax.axis_index("col")
    L = C // 2
    line = lax.div(c, 2)
    y = lax.rem(c, 2)
    mate = 2 * line + 1 - y
    c_next, c_prev = lax.rem(c + 1, C), lax.rem(c + C - 1, C)
    r_next, r_prev = lax.rem(r + 1, R), lax.rem(r + R - 1, R)
    can_up, can_down = line < L - 1, line > 0
    in_up, in_down = line < L - 2, line > 1
    at_end = jnp.logical_or(line == 0, line == L - 1)
    c_up, c_down = lax.rem(c + 2, C), lax.rem(c + C - 2, C)
    rows, cols = x.shape
    win = lr_in.shape[2]
    half = win // 2
    nr = rr_in.shape[0]
    nleft = lr_in.shape[0]
    pending = []
    fetch = pltpu.make_async_copy(x_in, x, x_s)
    owns = [pltpu.make_async_copy(a, b, o_s.at[n]) for n, (a, b) in enumerate(
        ((rr_in, rr.at[r]), (ro_in, ro.at[r]), (lr_in, lr.at[c]), (lo_in, lo.at[c])))]
    for copy in [owns[0], fetch] + owns[1:]:
        copy.start()

    around = functools.reduce(jnp.logical_or, [c == 0, c == 2, c == C - 3, c == C - 1])
    via = jnp.where(c == 0, C - 3, jnp.where(c == 2, 3, jnp.where(c == C - 3, C - 4, 2)))
    low_relay = jnp.logical_or(c == 2, c == 3)
    relays = jnp.logical_or(low_relay, jnp.logical_or(c == C - 4, c == C - 3))
    onward = jnp.where(low_relay, c_down, c_up)

    def put(src, dst, ssem, rsem, dev, pred=None):
        def copy():
            return pltpu.make_async_remote_copy(
                src_ref=src(), dst_ref=dst(), send_sem=ssem(), recv_sem=rsem(),
                device_id=dev, device_id_type=MESH,
            )

        run(pred, lambda: copy().start())
        pending.append((pred, lambda: copy().wait_send()))

    def got(dst, rsem, pred=None):
        def wait():
            pltpu.make_async_remote_copy(
                src_ref=dst(), dst_ref=dst(), send_sem=rsem(), recv_sem=rsem(),
                device_id={"col": c_next}, device_id_type=MESH,
            ).wait_recv()

        run(pred, wait)

    barrier = pltpu.get_barrier_semaphore()

    def greet(dev, pred=None):
        run(pred, lambda: pl.semaphore_signal(barrier, inc=1, device_id=dev, device_id_type=MESH))

    first, final = c == 0, c == C - 1
    for d in range(1, R):
        greet({"row": lax.rem(r + d, R)})
    greet({"col": c_next}, jnp.logical_not(final))
    greet({"col": c_prev}, jnp.logical_not(first))
    greet({"col": c_up}, can_up)
    greet({"col": c_down}, can_down)
    callers = R + 1 + jnp.where(can_up, 1, 0) + jnp.where(can_down, 1, 0)
    pl.semaphore_wait(barrier, callers - jnp.where(jnp.logical_or(first, final), 1, 0))

    def word(n, along, heard, c_to):
        run(both(along, heard), lambda: pl.semaphore_wait(tok.at[n], 1))
        run(along, lambda: pl.semaphore_signal(
            tok.at[n], inc=1, device_id={"col": c_to}, device_id_type=MESH))

    def far_ends():
        word(0, both(y == 0, line >= 1), line >= 2, jnp.where(can_up, c_up, mate))
        word(1, both(y == 1, line <= L - 2), line <= L - 3, jnp.where(can_down, c_down, mate))
        run(final, lambda: pl.semaphore_wait(tok.at[0], 1))
        run(first, lambda: pl.semaphore_wait(tok.at[1], 1))

    peers = [lax.rem(r + 2 * d, R) for d in range(1, R // 2)]
    sib = r + 1 - 2 * lax.rem(r, 2)

    def round_rows(src, buf, ss, rs):
        for d, q in enumerate(peers):
            put(src, lambda: buf.at[r], lambda d=d: ss.at[d], lambda: rs.at[r], {"row": q})
        put(src, lambda: buf.at[r], lambda: ss.at[R // 2 - 1], lambda: rs.at[r], {"row": sib})

    def to_sibling(buf, ss, rs):
        for d, q in enumerate(peers):
            got(lambda: buf.at[q], lambda: rs.at[q])
            put(lambda q=q: buf.at[q], lambda q=q: buf.at[q], lambda d=d: ss.at[R // 2 + d],
                lambda q=q: rs.at[q], {"row": sib})

    def from_sibling(buf, rs):
        for q in [sib] + [lax.rem(sib + 2 * d, R) for d in range(1, R // 2)]:
            got(lambda: buf.at[q], lambda: rs.at[q])

    class Gather:
        def __init__(self, own, buf, ss, rs):
            self.own, self.buf, self.ss, self.rs = own, buf, ss, rs
            self.waited = []

        def send(self, j, w, k, pred, own=False):
            src = (lambda: self.own.at[w]) if own else (lambda: self.buf.at[j, w])
            put(src, lambda: self.buf.at[j, w], lambda: self.ss.at[k, j, w],
                lambda: self.rs.at[j, w], {"col": (c_up, c_down, mate)[k]}, pred)

        def wait(self, j, w, pred=None):
            got(lambda: self.buf.at[j, w], lambda: self.rs.at[j, w], pred)

    lr_g = Gather(lr_in, lr, lr_s, lr_r)
    lo_g = Gather(lo_in, lo, lo_s, lo_r)

    def source(side, d, own):
        plane = line - d if side == 0 else line + d
        has = plane >= 0 if side == 0 else plane <= L - 1
        return lax.rem(2 * plane + (y if own else 1 - y) + 2 * C, C), has

    def onwards(g, side, d, own, w):
        can, inner = ((can_up, in_up), (can_down, in_down))[side]
        j, has = source(side, d, own)
        reach = can if own or g is lr_g else inner
        direct = g is lo_g and w >= nleft - DIRECT
        if direct and not own:
            other_end = line - d == 0 if side == 0 else line + d == L - 1
            reach = jnp.logical_or(inner, both(other_end, can))
        along = both(has, reach)
        across = None
        if own and ((g is lo_g and not (direct and d == L - 1)) or (g is lr_g and d == 1 and w < SHORT)):
            across = both(has, at_end)
        return j, has, along, across

    def nl_put(j, pred, own=False):
        src = lo_in.at[0, :, pl.ds(0, half)] if own else None
        put(lambda: src if own else lo.at[j, 0, :, pl.ds(0, half)], lambda: nl.at[j],
            lambda: nl_s.at[j], lambda: nl_r.at[j], {"row": r_prev}, pred)

    def relay(g, d, own, w):
        for side in (0, 1):
            if d == L - 1:
                use = jnp.bool_(False)
            j, has, along, across = onwards(g, side, d, own, w)
            use = along if across is None else jnp.logical_or(along, across)
            if d == L - 1 and across is None:
                continue
            g.wait(j, w, use)
            g.send(j, w, side, along)
            if across is not None:
                g.send(j, w, 2, across)
            if g is lo_g and w == 0:
                nl_put(j, use)

    def settle(g, w):
        for d in range(1, L):
            for own in (True, False):
                for side in (0, 1):
                    j, has, along, across = onwards(g, side, d, own, w)
                    use = along if across is None else jnp.logical_or(along, across)
                    rest = has if d == L - 1 and across is None else both(has, jnp.logical_not(use))
                    g.wait(j, w, rest)
                    if g is lo_g and w == 0:
                        nl_put(j, rest)

    round_rows(lambda: rr_in, rr, rr_s, rr_r)
    for w in range(nleft):
        lr_g.send(c, w, 2, None, True)
        lr_g.send(c, w, 0, can_up, True)
        lr_g.send(c, w, 1, can_down, True)
    far_ends()
    put(lambda: ro_in.at[0, :, pl.ds(0, half)], lambda: nx.at[r], lambda: nx_s.at[R - 1],
        lambda: nx_r.at[r], {"col": c_prev})
    round_rows(lambda: ro_in, ro, ro_s, ro_r)
    for w in range(nleft):
        lo_g.send(c, w, 2, None, True)
    nl_put(c, None, True)
    for copy in owns:
        copy.wait()

    for w in range(nleft):
        lr_g.wait(mate, w)
        lr_g.send(mate, w, 0, in_up if w < SHORT else can_up)
        lr_g.send(mate, w, 1, in_down if w < SHORT else can_down)
        relay(lr_g, 1, True, w)
    to_sibling(rr, rr_s, rr_r)
    from_sibling(rr, rr_r)
    for w in range(nr):
        h, l = split(rr[:, w].reshape(win, win))
        rr_h[w] = h
        rr_l[w] = l
    n_chunks = rows // chunk
    odd = lax.rem(r, 2)

    def turn(i, n):
        return i + odd * (n - 1 - 2 * i)

    def span(i):
        return pl.ds(pl.multiple_of(i * chunk, chunk), chunk)

    def halo(i, forward, n=None):
        cut = pl.ds(cols - half, half) if forward else pl.ds(0, half)
        dst, ss, rs = (hp, hp_s, hp_r) if forward else (hn, hn_s, hn_r)
        if n is None:
            return pltpu.make_async_remote_copy(
                src_ref=m.at[span(i), cut], dst_ref=dst.at[span(i), :],
                send_sem=ss.at[i], recv_sem=rs.at[i],
                device_id={"col": c_next if forward else c_prev}, device_id_type=MESH)
        return pltpu.make_async_remote_copy(
            src_ref=m.at[span(i), cut], dst_ref=hx.at[n],
            send_sem=ss.at[i], recv_sem=hx_r.at[n],
            device_id={"col": via}, device_id_type=MESH)

    def far_start(i, n):
        for forward in (True, False):
            far = y == (1 if forward else 0)
            if n is None:
                run(far, lambda: halo(i, forward).start())
            else:
                run(both(far, around), lambda: halo(i, forward, n).start())
                run(both(far, jnp.logical_not(around)), lambda: halo(i, forward).start())

    def near_start(i):
        for forward in (True, False):
            run(y == (0 if forward else 1), lambda: halo(i, forward).start())

    def right_chunk(i):
        for w in range(nr):
            a = split(x[span(i), pl.ds(w * win, win)])
            m[span(i), pl.ds(w * win, win)] = dot3(a, (rr_h[w], rr_l[w]), RIGHT)

    fetch.wait()
    for n in range(n_chunks):
        i = turn(n, n_chunks)
        right_chunk(i)
        far_start(i, n if n < detour else None)
        if n >= detour:
            near_start(i)
        if n == detour - 1:
            for k in range(detour):
                near_start(turn(k, n_chunks))

    def hx_copy(n):
        i = turn(n, n_chunks)
        even = pltpu.make_async_remote_copy(
            src_ref=hx.at[n], dst_ref=hp.at[span(i), :], send_sem=hx_s.at[n], recv_sem=hp_r.at[i],
            device_id={"col": onward}, device_id_type=MESH)
        uneven = pltpu.make_async_remote_copy(
            src_ref=hx.at[n], dst_ref=hn.at[span(i), :], send_sem=hx_s.at[n], recv_sem=hn_r.at[i],
            device_id={"col": onward}, device_id_type=MESH)
        return even, uneven

    def hx_relay(n):
        got(lambda: hx.at[n], lambda: hx_r.at[n], relays)
        even, uneven = hx_copy(n)
        run(both(relays, y == 0), even.start)
        run(both(relays, y == 1), uneven.start)

    got(lambda: nx.at[r], lambda: nx_r.at[r])
    round_rows(lambda: nx.at[r], nx, nx_s, nx_r)
    for w in range(nleft):
        relay(lr_g, 1, False, w)
    for w in range(nleft):
        lo_g.send(c, w, 0, can_up, True)
        lo_g.send(c, w, 1, can_down, True)
    to_sibling(ro, ro_s, ro_r)
    to_sibling(nx, nx_s, nx_r)
    for n in range(detour):
        hx_relay(n)
    for d in range(2, L):
        for own in (True, False):
            for w in range(nleft):
                relay(lr_g, d, own, w)

    def lo_mate(w):
        lo_g.wait(mate, w)
        lo_g.send(mate, w, 0, in_up)
        lo_g.send(mate, w, 1, in_down)
        if w == 0:
            nl_put(mate, None)

    from_sibling(ro, ro_r)
    from_sibling(nx, nx_r)
    for w in range(nr):
        h, l = split(ro[:, w].reshape(win, win))
        ro_h[w] = h
        ro_l[w] = l
    h, l = split(nx[...].reshape(win, half))
    nx_h[...] = h
    nx_l[...] = l
    for w in range(nleft):
        lo_mate(w)

    def shifted_chunk(i):
        got(lambda: hp.at[span(i), :], lambda: hp_r.at[i])
        first = split(m[span(i), pl.ds(0, half)])
        ahead = split(hp[span(i), :])
        top = (ro_h[0, :half, half:], ro_l[0, :half, half:])
        low = (ro_h[0, half:, half:], ro_l[0, half:, half:])
        m2[span(i), pl.ds(0, half)] = dot3(ahead, top, RIGHT) + dot3(first, low, RIGHT)
        for w in range(1, nr):
            a = split(m[span(i), pl.ds(w * win - half, win)])
            m2[span(i), pl.ds(w * win - half, win)] = dot3(a, (ro_h[w], ro_l[w]), RIGHT)
        got(lambda: hn.at[span(i), :], lambda: hn_r.at[i])
        last = split(m[span(i), pl.ds(cols - half, half)])
        after = split(hn[span(i), :])
        top = (nx_h[:half, :], nx_l[:half, :])
        low = (nx_h[half:, :], nx_l[half:, :])
        m2[span(i), pl.ds(cols - half, half)] = dot3(last, top, RIGHT) + dot3(after, low, RIGHT)

    per = win // chunk

    def left_window(k):
        k = turn(k, nleft)
        at = pl.ds(pl.multiple_of(k * win, win), win)
        q = split(lr[:, k].reshape(win, win))
        for w in range(cols // win):
            across = pl.ds(w * win, win)
            m3[at, across] = dot3(q, split(m2[at, across]), LEFT)

    def rows_up(pred):
        put(lambda: m3.at[pl.ds(rows - half, half), :], lambda: ha, lambda: hr_s.at[0],
            lambda: hr_r.at[0], {"row": r_next}, pred)

    def rows_down(pred):
        put(lambda: m3.at[pl.ds(0, half), :], lambda: hb, lambda: hr_s.at[1],
            lambda: hr_r.at[1], {"row": r_prev}, pred)

    for n in range(per):
        shifted_chunk(turn(n, n_chunks))
    for own in (True, False):
        relay(lo_g, 1, own, 0)
    for w in range(nleft):
        settle(lr_g, w)
    left_window(0)
    rows_down(odd == 0)
    rows_up(odd == 1)
    for w in range(1, nleft):
        for own in (True, False):
            relay(lo_g, 1, own, w)
    for k in range(1, nleft):
        for n in range(k * per, (k + 1) * per):
            shifted_chunk(turn(n, n_chunks))
        left_window(k)
    rows_up(odd == 0)
    rows_down(odd == 1)
    for w in range(nleft):
        for d in range(2, L):
            for own in (True, False):
                relay(lo_g, d, own, w)

    strip = win // C

    def store(q, parts, at, add):
        res = dot3(split(q), split(jnp.concatenate(parts, axis=0)), LEFT)
        out[at, :] = out[at, :] + res if add else res

    settle(lo_g, 0)
    got(lambda: ha, lambda: hr_r.at[0])
    store(lo[:, 0, :, half:].reshape(win, half), [ha[...], m3[pl.ds(0, half), :]],
          pl.ds(0, half), False)
    for j in range(C):
        got(lambda: nl.at[j], lambda: nl_r.at[j])
    got(lambda: hb, lambda: hr_r.at[1])
    store(nl[...].reshape(win, half), [m3[pl.ds(rows - half, half), :], hb[...]],
          pl.ds(rows - half, half), False)
    for w in range(1, nleft):
        settle(lo_g, w)
        base = w * win - half
        store(lo[:, w].reshape(win, win), [m3[pl.ds(base, win), :]], pl.ds(base, win), False)

    for n in range(n_chunks):
        i = turn(n, n_chunks)
        for forward in (True, False):
            halo(i, forward).wait_send()
        if n < detour:
            run(relays, hx_copy(n)[0].wait_send)
    for pred, wait in pending:
        run(pred, wait)


def solution(mesh):
    R, C = mesh.shape["row"], mesh.shape["col"]

    def body(schur, left_rot, right_rot, left_off, right_off):
        rows, cols = schur.shape
        win = left_rot.shape[2]
        half = win // 2
        nr, nleft = right_rot.shape[0], left_rot.shape[0]
        chunk = half
        n_chunks = rows // chunk
        dma = pltpu.SemaphoreType.DMA
        vm = pltpu.VMEM
        right = (R,) + right_rot.shape
        left = (C,) + left_rot.shape
        return pl.pallas_call(
            functools.partial(kernel, R, C, chunk, DETOUR),
            out_shape=jax.ShapeDtypeStruct((rows, cols), F32),
            in_specs=[pl.BlockSpec(memory_space=pltpu.HBM)] * 5,
            out_specs=pl.BlockSpec(memory_space=vm),
            scratch_shapes=[
                vm((rows, cols), F32), vm(right, F32), vm(right, F32), vm((R, win // R, half), F32),
                vm(left, F32), vm(left, F32), vm((C, win // C, half), F32),
                vm((rows, cols), F32), vm((rows, cols), F32), vm((rows, cols), F32),
                vm((rows, half), F32), vm((rows, half), F32),
                vm((max(DETOUR, 1), chunk, half), F32),
                vm((half, cols), F32), vm((half, cols), F32),
                vm((nr, win, win), BF16), vm((nr, win, win), BF16),
                vm((nr, win, win), BF16), vm((nr, win, win), BF16),
                vm((win, half), BF16), vm((win, half), BF16),
                dma((R,)), dma((R,)), dma((R,)), dma((R,)), dma((R,)), dma((R,)),
                dma((3, C, nleft)), dma((C, nleft)), dma((3, C, nleft)), dma((C, nleft)), dma((C,)), dma((C,)),
                dma((n_chunks,)), dma((n_chunks,)), dma((n_chunks,)), dma((n_chunks,)),
                dma((max(DETOUR, 1),)), dma((max(DETOUR, 1),)),
                dma((2,)), dma((2,)), dma, dma((4,)), pltpu.SemaphoreType.REGULAR((2,)),
            ],
            compiler_params=pltpu.CompilerParams(collective_id=0, has_side_effects=True, vmem_limit_bytes=44 * 2**20),
        )(*(pltpu.with_memory_space_constraint(a, pltpu.HBM) for a in (schur, right_rot, right_off, left_rot, left_off)))

    return jax.shard_map(
        body,
        mesh=mesh,
        in_specs=(
            P("row", "col"),
            P("row", "col", None),
            P("col", "row", None),
            P("row", "col", None),
            P("col", "row", None),
        ),
        out_specs=P("row", "col"),
        check_vma=False,
    )
```
